32 devices in a mesh: col: 4 (over y, x), row: 8 (over z, core).
Axes of the slice: x: 2, y: 2, z: 4, core: 2. Of those that a mesh axis runs over, the one named last changes fastest.
Arguments:
- covariance: float32 [12288, 12288], P('row', 'col'), may hold values from -2 to 2, as said below
- wfs_map: int32 [12288], P('row'), may hold values from 0 to 5
- noise_var: float32 [6], replicated, may hold values from 0.5 to 2
- targets: float32 [12288, 2048], P('row', 'col'), may hold values from -0.6 to 0.6
- target_pos: float32 [2, 2048], replicated, may hold values from -1 to 1
- layer_strength: float32 [35], replicated, may hold values from 0.005 to 0.05
- layer_scale: float32 [35], replicated, may hold values from 0.2 to 2
- tile_layer: int32 [16], replicated, may hold values from 0 to 34
Outputs:
- updated: float32 [12288, 12288], P('row', 'col')
- panel_factor: float32 [12288, 256], P('row')
- reconstructor: float32 [12288, 2048], P('row', 'col')
- error_cov: float32 [2048, 2048], P('row', 'col')
The draws below stay inside these ranges and needn't reach their ends.
Inputs may be any that keep to these rules, and one draw needn't show every extreme that they name: `covariance`: symmetric and positive semidefinite; its diagonal lies between 0.5 and 2.
All inputs are finite; a program needn't handle non-finite values.
Results may differ from the reference program's by a relative error of at most 0.0003.
Values sent between devices are 32-bit elements; how exact they have to be, the bound alone decides.
A program may use at most 128 MiB of HBM per device.

```python
import math
import jax
import jax.numpy as jnp
from jax import lax

M = 12288
PB = 256
TC = 2048
TILE = 128
NL = 35
NWFS = 6


def draw_covariance(key, part):
    key_base = jax.random.fold_in(key, 11)
    indices = jnp.arange(M, dtype=jnp.int32)
    base_draw = jax.random.normal(key_base, (M, PB), jnp.float32)
    row_scale = jnp.ones((M,), jnp.float32)
    smooth = base_draw
    weight = 1.0
    for lag in range(1, 8):
        weight = weight * 0.8
        smooth = smooth + weight * jnp.roll(base_draw, lag, axis=0)
    gram = jnp.dot(smooth, smooth.T, precision=lax.Precision.HIGHEST)
    norms = jnp.sum(smooth * smooth, axis=1)
    inverse = row_scale / jnp.sqrt(norms)
    gram = gram * inverse[:, None] * inverse[None, :]
    symmetric = jnp.where(indices[:, None] >= indices[None, :], gram, gram.T)
    symmetric = jnp.clip(symmetric, -2.0, 2.0)
    return symmetric.at[indices, indices].set(row_scale)


def place_ends(entries, stream_key, smallest, high):
    extent = entries.shape
    spot = [jax.random.randint(jax.random.fold_in(stream_key, axis), (), 0, extent[axis]) for axis in range(len(extent))]
    entries = entries.at[tuple(spot)].set(smallest)
    longest = extent.index(max(extent))
    spot[longest] = (spot[longest] + 1) % extent[longest]
    return entries.at[tuple(spot)].set(high)


def steps_of(key, shape, split, smallest, high):
    factor_of = 1.0
    for dim, blocks in split:
        steps = jax.random.uniform(jax.random.fold_in(jax.random.fold_in(key, 6), dim), (blocks,), jnp.float32, smallest / len(split), high / len(split))
        factor_of = factor_of * jnp.repeat(jnp.exp(steps), shape[dim] // blocks).reshape((-1,) + (1,) * (len(shape) - 1 - dim))
    return factor_of


def bell_draw(stream_key, extent, scale, most, pieces=(), kind=jnp.bfloat16):
    result = scale * jax.random.normal(stream_key, extent, jnp.float32)
    if pieces:
        result = result * steps_of(stream_key, extent, pieces, -0.22, 0.18)
    return jnp.clip(result, -most, most).astype(kind)


def setup_inputs(seed: int = 0) -> dict:
    streams_of = jax.random.split(jax.random.key(seed), 9)
    covariance = draw_covariance(jax.random.fold_in(streams_of[8], 71), 0)
    wfs_map = place_ends(jax.random.randint(streams_of[1], (M,), 0, NWFS), jax.random.fold_in(streams_of[1], 1), 0, NWFS - 1).astype(jnp.int32)
    noise_var = jnp.clip(jnp.exp(jax.random.uniform(streams_of[2], (NWFS,), jnp.float32, math.log(0.5), math.log(2.0))), 0.5, 2.0)
    targets = bell_draw(streams_of[3], (M, TC), 0.1, 0.6, ((0, 8), (1, 4)), jnp.float32)
    target_pos = jnp.clip(jax.random.uniform(streams_of[4], (2, TC), jnp.float32, -1.0, 1.0), -1.0, 1.0)
    layer_strength = jnp.clip(jnp.exp(jax.random.uniform(streams_of[5], (NL,), jnp.float32, math.log(0.005), math.log(0.05))), 0.005, 0.05)
    layer_scale = jnp.clip(jnp.exp(jax.random.uniform(streams_of[6], (NL,), jnp.float32, math.log(0.2), math.log(2.0))), 0.2, 2.0)
    tile_layer = place_ends(jax.random.randint(streams_of[7], (TC // TILE,), 0, NL), jax.random.fold_in(streams_of[7], 1), 0, NL - 1).astype(jnp.int32)
    return dict(covariance=covariance, wfs_map=wfs_map, noise_var=noise_var, targets=targets, target_pos=target_pos, layer_strength=layer_strength, layer_scale=layer_scale, tile_layer=tile_layer)


precise = lax.Precision.HIGHEST

def target_covariance(pos_rows, pos_cols, layer_rows, layer_cols, layer_strength, layer_scale):
    distance = (pos_rows[0][:, None] - pos_cols[0][None, :]) ** 2 + (pos_rows[1][:, None] - pos_cols[1][None, :]) ** 2
    lowest = jnp.minimum(layer_rows[:, None], layer_cols[None, :])
    levels = jnp.arange(layer_strength.shape[0], dtype=jnp.int32)
    weights = layer_strength[:, None, None] / (1.0 + distance[None] / (layer_scale * layer_scale)[:, None, None])
    return jnp.sum(jnp.where(levels[:, None, None] <= lowest[None], weights, 0.0), axis=0)

def reference(covariance, wfs_map, noise_var, targets, target_pos, layer_strength, layer_scale, tile_layer):
    indices = jnp.arange(M, dtype=jnp.int32)
    matrix = covariance.at[indices, indices].add(noise_var[wfs_map])
    factor = jnp.linalg.cholesky(matrix[:PB, :PB])
    solved = jax.scipy.linalg.solve_triangular(factor, matrix[:, :PB].T, lower=True).T
    top_rows = jnp.concatenate([factor, jnp.zeros((M - PB, PB), jnp.float32)], axis=0)
    panel_factor = jnp.where(indices[:, None] < PB, top_rows, solved)
    block_rows = M // 16

    def update_block(block):
        start = (block * block_rows).astype(jnp.int32)
        rows_here = lax.dynamic_slice_in_dim(panel_factor, start, block_rows, 0)
        matrix_here = lax.dynamic_slice_in_dim(matrix, start, block_rows, 0)
        row_ids = start + jnp.arange(block_rows, dtype=jnp.int32)
        product = jnp.dot(rows_here, panel_factor.T, precision=precise)
        fill_cols = jnp.concatenate([rows_here, jnp.zeros((block_rows, M - PB), jnp.float32)], axis=1)
        trailing = (row_ids[:, None] >= PB) & (indices[None, :] >= PB)
        return jnp.where(trailing, matrix_here - product, jnp.where(indices[None, :] < PB, fill_cols, 0.0))
    updated = lax.map(update_block, jnp.arange(16, dtype=jnp.int32)).reshape(M, M)
    head_rows = jax.scipy.linalg.solve_triangular(factor, targets[:PB], lower=True)
    head_top = jnp.concatenate([head_rows, jnp.zeros((M - PB, TC), jnp.float32)], axis=0)
    reduced = targets - jnp.dot(panel_factor, head_rows, precision=precise)
    reconstructor = jnp.where(indices[:, None] < PB, head_top, reduced)
    layer_all = jnp.repeat(tile_layer, TILE)

    def covariance_block(block):
        start = (block * TILE).astype(jnp.int32)
        return target_covariance(lax.dynamic_slice_in_dim(target_pos, start, TILE, 1), target_pos, lax.dynamic_slice_in_dim(layer_all, start, TILE, 0), layer_all, layer_strength, layer_scale)
    target_cov = lax.map(covariance_block, jnp.arange(TC // TILE, dtype=jnp.int32)).reshape(TC, TC)
    error_cov = target_cov - jnp.dot(head_rows.T, head_rows, precision=precise)
    return (updated, panel_factor, reconstructor, error_cov)
```

```python
import functools

import jax
import jax.numpy as jnp
from jax import lax
from jax.experimental import pallas as pl
from jax.experimental.pallas import tpu as pltpu
from jax.sharding import PartitionSpec as P

PB = 256
TILE = 128
HALF = PB // 2
ROWS = 128
CHUNKS = 8
ROW_CHUNKS = 6
SEGMENT = 16

MESH = pl.DeviceIdType.MESH
precise = lax.Precision.HIGHEST


def dot(a, b, dims=((1,), (0,))):
    return lax.dot_general(
        a, b, (dims, ((), ())), precision=precise, preferred_element_type=jnp.float32
    )


def chunks_of(count):
    return max(n for n in range(1, CHUNKS + 1) if count // 128 % n == 0)


def split(x):
    high = x.astype(jnp.bfloat16)
    return high, (x - high.astype(jnp.float32)).astype(jnp.bfloat16)


def dot_split(a, b):
    total = jnp.dot(a[0], b[0], preferred_element_type=jnp.float32)
    total += jnp.dot(a[1], b[0], preferred_element_type=jnp.float32)
    return total + jnp.dot(a[0], b[1], preferred_element_type=jnp.float32)


def target_covariance(pos_rows, pos_cols, layer_rows, layer_cols, layer_strength, layer_scale):
    distance = (pos_rows[0][:, None] - pos_cols[0][None, :]) ** 2 + (
        pos_rows[1][:, None] - pos_cols[1][None, :]
    ) ** 2
    lowest = jnp.minimum(layer_rows[:, None], layer_cols[None, :])
    levels = jnp.arange(layer_strength.shape[0], dtype=jnp.int32)
    weights = layer_strength[:, None, None] / (
        1.0 + distance[None] / (layer_scale * layer_scale)[:, None, None]
    )
    return jnp.sum(jnp.where(levels[:, None, None] <= lowest[None], weights, 0.0), axis=0)


def gray_neighbours(c, n):
    position = c * 0
    after = c * 0
    before = c * 0
    ring = [i ^ (i >> 1) for i in range(n)]
    for i, node in enumerate(ring):
        position = jnp.where(c == node, i, position)
        after = jnp.where(c == node, ring[(i + 1) % n], after)
        before = jnp.where(c == node, ring[(i - 1) % n], before)
    return position, after, before


def pivots(s_ref, m_ref, r_ref, start, count):
    n = s_ref.shape[0]
    lanes = lax.broadcasted_iota(jnp.int32, (n, n), 1)
    lane = lax.broadcasted_iota(jnp.int32, (1, n), 1)
    down = lax.broadcasted_iota(jnp.int32, (n, 1), 0)

    def step(k, carry):
        row = s_ref[pl.ds(k, 1), :]
        inverse_row = m_ref[pl.ds(k, 1), :]
        whole = s_ref[...]
        column = jnp.sum(jnp.where(lanes == k, whole, 0.0), axis=1, keepdims=True)
        pivot = jnp.sum(jnp.where(lane == k, row, 0.0), axis=1, keepdims=True)
        root = lax.rsqrt(pivot)
        factor = jnp.where(down > k, column * (1.0 / pivot), 0.0)
        r_ref[pl.ds(k, 1), :] = jnp.where(lane >= k, row * root, 0.0)
        s_ref[...] = whole - factor * row
        scaled = m_ref[...] - factor * inverse_row
        m_ref[...] = jnp.where(down == k, scaled * root, scaled)
        return carry

    lax.fori_loop(start, start + count, step, 0)


def exchange_kernel(
    n_row,
    n_col,
    cov,
    targets,
    diag,
    row_raw,
    col_raw,
    head_raw,
    need_raw,
    factor_ref,
    inverse_ref,
    blocks,
    s_ref,
    m_ref,
    r_ref,
    local_sem,
    diag_send,
    diag_recv,
    col_send,
    col_recv,
    row_send,
    row_recv,
    need_send,
    need_recv,
):
    r = lax.axis_index("row")
    c = lax.axis_index("col")
    row_count = row_raw.shape[0]
    col_count = col_raw.shape[1]
    width = head_raw.shape[1]
    need = need_raw.shape[1]
    col_chunks = chunks_of(col_count)
    even = lax.rem(r, 2) == 0
    place, after, before = gray_neighbours(c, n_col)
    far_row = jnp.minimum(r + 2, n_row - 1)
    near_row = jnp.where(even, r + 1, r - 1)

    head_copy = pltpu.make_async_copy(targets.at[pl.ds(0, PB), :], head_raw, local_sem.at[0])
    col_copy = pltpu.make_async_copy(cov.at[pl.ds(0, PB), :], col_raw, local_sem.at[1])
    row_copy = pltpu.make_async_copy(cov.at[:, pl.ds(0, PB)], row_raw, local_sem.at[2])
    pl.when(r == 0)(lambda: (head_copy.start(), col_copy.start(), None)[-1])
    pl.when(c == 0)(lambda: (row_copy.start(), None)[-1])

    barrier = pltpu.get_barrier_semaphore()
    for k in range(1, n_row):
        pl.semaphore_signal(
            barrier, inc=1, device_id=(c, lax.rem(r + k, n_row)), device_id_type=MESH
        )
    for k in range(1, n_col):
        pl.semaphore_signal(
            barrier, inc=1, device_id=(lax.rem(c + k, n_col), r), device_id_type=MESH
        )
    pl.semaphore_wait(barrier, n_row + n_col - 2)

    def remote(src, dst, send, recv, col, row):
        return pltpu.make_async_remote_copy(
            src_ref=src,
            dst_ref=dst,
            send_sem=send,
            recv_sem=recv,
            device_id=(col, row),
            device_id_type=MESH,
        )

    def chain(src, dst, send, recv):
        return (
            remote(src, dst, send.at[0], recv, c, far_row),
            remote(src, dst, send.at[1], recv, c, near_row),
        )

    def chain_start(copies, allowed):
        pl.when(allowed & even & (r + 2 < n_row))(lambda: (copies[0].start(), None)[-1])
        pl.when(allowed & even & (r + 1 < n_row))(lambda: (copies[1].start(), None)[-1])

    def chain_end(copies, allowed):
        pl.when(allowed & even & (r + 2 < n_row))(lambda: (copies[0].wait_send(), None)[-1])
        pl.when(allowed & even & (r + 1 < n_row))(lambda: (copies[1].wait_send(), None)[-1])

    quarters = [(0, 0), (HALF, 0), (HALF, HALF)]

    def diag_chain(i, source):
        dst = blocks.at[i]
        src = dst
        if source:
            src = diag.at[pl.ds(quarters[i][0], HALF), pl.ds(quarters[i][1], HALF)]
        return src, dst

    def diag_copies(i, source):
        src, dst = diag_chain(i, source)
        down = chain(src, dst, diag_send.at[i], diag_recv.at[i])
        across = [
            remote(src, dst, diag_send.at[i, 1 + k], diag_recv.at[i], k, r)
            for k in range(1, n_col)
        ]
        return down, across

    def diag_start(i, source, allowed):
        down, across = diag_copies(i, source)
        chain_start(down, allowed)
        for copy in across:
            pl.when(allowed)(lambda copy=copy: (copy.start(), None)[-1])

    def diag_wait(i):
        @pl.when((r > 0) | (c > 0))
        def _():
            diag_copies(i, False)[0][0].wait_recv()

    first = (r == 0) & (c == 0)
    for i in range(3):
        diag_start(i, True, first)

    chunk = col_count // col_chunks

    def col_copies(j, source):
        if j == 0:
            src = targets.at[pl.ds(0, PB), :] if source else head_raw
            return chain(src, head_raw, col_send.at[j], col_recv.at[j])
        columns = pl.ds((j - 1) * chunk, chunk)
        dst = col_raw.at[:, columns]
        src = cov.at[pl.ds(0, PB), columns] if source else dst
        return chain(src, dst, col_send.at[j], col_recv.at[j])

    def col_forward(j):
        @pl.when(r > 0)
        def _():
            col_copies(j, False)[0].wait_recv()

        chain_start(col_copies(j, False), r > 0)

    for i in range(3):
        diag_wait(i)
        diag_start(i, False, (r > 0) & (c == 0))

    for j in range(col_chunks + 1):
        chain_start(col_copies(j, True), r == 0)

    step_rows = row_count // (2 * ROW_CHUNKS)

    def row_copies(j, way, source):
        rows = pl.ds((2 * j + way) * step_rows, step_rows)
        dst = row_raw.at[rows, :]
        src = cov.at[rows, pl.ds(0, PB)] if source else dst
        to = after if way == 0 else before
        return remote(src, dst, row_send.at[j, way], row_recv.at[j, way], to, r)

    def forwards(way):
        return (place > 0) & ((place < n_col - 1) if way == 0 else (place > 1))

    def row_forward(j):
        for way in range(2):
            copy = row_copies(j, way, False)
            pl.when(place > 0)(lambda copy=copy: (copy.wait_recv(), None)[-1])
            pl.when(forwards(way))(lambda copy=copy: (copy.start(), None)[-1])

    for j in range(ROW_CHUNKS):
        for way in range(2):
            copy = row_copies(j, way, True)
            pl.when(place == 0)(lambda copy=copy: (copy.start(), None)[-1])

    owner = lax.div(r * need, width)
    offset = pl.multiple_of(lax.rem(r * need, width), 128)
    need_copies = [
        remote(
            head_raw.at[:, pl.ds(offset, need)], need_raw, need_send.at[k], need_recv, k, r
        )
        for k in range(n_col)
    ]
    own_need = pltpu.make_async_copy(
        head_raw.at[:, pl.ds(offset, need)], need_raw, local_sem.at[3]
    )

    def need_start():
        pl.when(r == 0)(lambda: (head_copy.wait(), None)[-1])
        for k in range(n_col):
            pl.when((c == owner) & (c != k))(lambda k=k: (need_copies[k].start(), None)[-1])
        pl.when(c == owner)(lambda: (own_need.start(), None)[-1])

    @pl.when(first)
    def _():
        for i in range(3):
            blocks[i] = diag[pl.ds(quarters[i][0], HALF), pl.ds(quarters[i][1], HALF)]

    unit = (
        lax.broadcasted_iota(jnp.int32, (HALF, HALF), 0)
        == lax.broadcasted_iota(jnp.int32, (HALF, HALF), 1)
    ).astype(jnp.float32)
    events = [lambda: (col_forward(0), need_start())]
    for j in range(max(col_chunks, ROW_CHUNKS)):
        if j < ROW_CHUNKS:
            events.append(lambda j=j: row_forward(j))
        if j < col_chunks:
            events.append(lambda j=j: col_forward(j + 1))

    def half(block, where):
        s_ref[...] = block
        m_ref[...] = unit
        for start in range(0, HALF, SEGMENT):
            pivots(s_ref, m_ref, r_ref, start, SEGMENT)
            if events:
                events.pop(0)()

    half(blocks[0], 0)
    inverse_11 = m_ref[...]
    inverse_ref[pl.ds(0, HALF), pl.ds(0, HALF)] = inverse_11
    inverse_ref[pl.ds(0, HALF), pl.ds(HALF, HALF)] = jnp.zeros((HALF, HALF), jnp.float32)
    factor_ref[pl.ds(0, HALF), pl.ds(0, HALF)] = r_ref[...].T
    factor_ref[pl.ds(0, HALF), pl.ds(HALF, HALF)] = jnp.zeros((HALF, HALF), jnp.float32)
    lower = dot(blocks[1], inverse_11, ((1,), (1,)))
    factor_ref[pl.ds(HALF, HALF), pl.ds(0, HALF)] = lower
    half(blocks[2] - dot(lower, lower, ((1,), (1,))), 1)
    inverse_22 = m_ref[...]
    inverse_ref[pl.ds(HALF, HALF), pl.ds(HALF, HALF)] = inverse_22
    factor_ref[pl.ds(HALF, HALF), pl.ds(HALF, HALF)] = r_ref[...].T
    lower = factor_ref[pl.ds(HALF, HALF), pl.ds(0, HALF)]
    inverse_ref[pl.ds(HALF, HALF), pl.ds(0, HALF)] = -dot(
        inverse_22, dot(lower, inverse_ref[pl.ds(0, HALF), pl.ds(0, HALF)])
    )
    while events:
        events.pop(0)()

    pl.when(c == owner)(lambda: (own_need.wait(), None)[-1])
    pl.when(c != owner)(lambda: (need_copies[0].wait_recv(), None)[-1])
    for k in range(n_col):
        pl.when((c == owner) & (c != k))(lambda k=k: (need_copies[k].wait_send(), None)[-1])
    for i in range(3):
        down, across = diag_copies(i, True)
        chain_end(down, c == 0)
        for copy in across:
            pl.when(c == 0)(lambda copy=copy: (copy.wait_send(), None)[-1])
    for j in range(col_chunks + 1):
        chain_end(col_copies(j, False), r >= 0)
    for j in range(ROW_CHUNKS):
        for way in range(2):
            copy = row_copies(j, way, False)
            pl.when((place == 0) | forwards(way))(lambda copy=copy: (copy.wait_send(), None)[-1])
    pl.when(r == 0)(lambda: (col_copy.wait(), None)[-1])
    pl.when(c == 0)(lambda: (row_copy.wait(), None)[-1])


def update_kernel(
    cov,
    row_raw,
    targets,
    noise,
    col_raw,
    head_raw,
    need_raw,
    factor,
    inverse,
    target_cov,
    updated,
    panel,
    reconstructor,
    error_cov,
    col_high,
    col_low,
    head,
    head_high,
    head_low,
):
    t = pl.program_id(0)
    r = lax.axis_index("row")
    c = lax.axis_index("col")
    rows, cols = cov.shape
    top = (r == 0) & (t < PB // rows)

    @pl.when(t == 0)
    def _():
        whole = inverse[...]
        col_high[...], col_low[...] = split(dot(whole, col_raw[...]))
        solved = dot(whole, head_raw[...])
        head[...] = solved
        head_high[...], head_low[...] = split(solved)
        other = dot(whole, need_raw[...])
        error_cov[...] = target_cov[...] - dot(other, solved, ((0,), (0,)))

    @pl.when(jnp.logical_not(top))
    def _():
        solved = dot(row_raw[...], inverse[...], ((1,), (1,)))
        panel[...] = solved
        left = split(solved)
        updated[...] = cov[...] - dot_split(left, (col_high[...], col_low[...]))
        reconstructor[...] = targets[...] - dot_split(left, (head_high[...], head_low[...]))
        start = r * (rows * pl.num_programs(0)) + t * rows - c * cols

        @pl.when((start >= 0) & (start < cols))
        def _():
            columns = pl.ds(pl.multiple_of(start, rows), rows)
            diagonal = lax.broadcasted_iota(jnp.int32, (rows, rows), 0) == (
                lax.broadcasted_iota(jnp.int32, (rows, rows), 1)
            )
            updated[:, columns] = updated[:, columns] + jnp.where(diagonal, noise[0], 0.0)

    @pl.when(top)
    def _():
        block = pl.ds(pl.multiple_of(jnp.minimum(t, PB // rows - 1) * rows, rows), rows)
        panel[...] = factor[block, :]
        updated[...] = jnp.zeros_like(updated)
        reconstructor[...] = head[block, :]

    @pl.when(c == 0)
    def _():
        updated[:, pl.ds(0, PB)] = panel[...]


def local(
    n_row, n_col, covariance, wfs_map, noise_var, targets, target_pos, layer_strength,
    layer_scale, tile_layer
):
    row_count, col_count = covariance.shape
    target_width = targets.shape[1]
    row_index = lax.axis_index("row")
    col_index = lax.axis_index("col")
    kinds = jnp.arange(noise_var.shape[0], dtype=jnp.int32)
    noise_rows = jnp.sum(
        jnp.where(wfs_map[None, :] == kinds[:, None], noise_var[:, None], 0.0), axis=0
    )
    diag = covariance[:PB, :PB] + jnp.where(
        jnp.arange(PB)[:, None] == jnp.arange(PB)[None, :], noise_rows[None, :PB], 0.0
    )
    error_rows = target_width * n_col // n_row
    col_chunks = chunks_of(col_count)
    row_start = row_index * error_rows
    col_start = col_index * target_width
    layer_all = jnp.repeat(tile_layer, TILE)
    target_cov = target_covariance(
        lax.dynamic_slice_in_dim(target_pos, row_start, error_rows, 1),
        lax.dynamic_slice_in_dim(target_pos, col_start, target_width, 1),
        lax.dynamic_slice_in_dim(layer_all, row_start, error_rows, 0),
        lax.dynamic_slice_in_dim(layer_all, col_start, target_width, 0),
        layer_strength,
        layer_scale,
    )

    def f32(*shape):
        return jax.ShapeDtypeStruct(shape, jnp.float32)

    vmem = pl.BlockSpec(memory_space=pltpu.VMEM)
    anywhere = pl.BlockSpec(memory_space=pl.ANY)
    dma = pltpu.SemaphoreType.DMA
    row_raw, col_raw, head_raw, need_raw, factor, inverse = pl.pallas_call(
        functools.partial(exchange_kernel, n_row, n_col),
        out_shape=(
            f32(row_count, PB),
            f32(PB, col_count),
            f32(PB, target_width),
            f32(PB, error_rows),
            f32(PB, PB),
            f32(PB, PB),
        ),
        in_specs=[anywhere, anywhere, vmem],
        out_specs=[vmem] * 6,
        scratch_shapes=[
            pltpu.VMEM((3, HALF, HALF), jnp.float32),
            pltpu.VMEM((HALF, HALF), jnp.float32),
            pltpu.VMEM((HALF, HALF), jnp.float32),
            pltpu.VMEM((HALF, HALF), jnp.float32),
            dma((4,)),
            dma((3, n_col + 1)),
            dma((3,)),
            dma((col_chunks + 1, 2)),
            dma((col_chunks + 1,)),
            dma((ROW_CHUNKS, 2)),
            dma((ROW_CHUNKS, 2)),
            dma((n_col,)),
            dma,
        ],
        compiler_params=pltpu.CompilerParams(
            collective_id=0, has_side_effects=True, vmem_limit_bytes=24 * 1024 * 1024
        ),
        name="exchange",
    )(covariance, targets, diag)

    def tiled(width):
        return pl.BlockSpec((ROWS, width), lambda t: (t, 0))

    def held(height, width):
        return pl.BlockSpec((height, width), lambda t: (0, 0))

    return pl.pallas_call(
        update_kernel,
        grid=(row_count // ROWS,),
        out_shape=(
            f32(row_count, col_count),
            f32(row_count, PB),
            f32(row_count, target_width),
            f32(error_rows, target_width),
        ),
        in_specs=[
            tiled(col_count),
            tiled(PB),
            tiled(target_width),
            pl.BlockSpec((1, 1, ROWS), lambda t: (t, 0, 0)),
            held(PB, col_count),
            held(PB, target_width),
            held(PB, error_rows),
            held(PB, PB),
            held(PB, PB),
            held(error_rows, target_width),
        ],
        out_specs=[
            tiled(col_count),
            tiled(PB),
            tiled(target_width),
            held(error_rows, target_width),
        ],
        scratch_shapes=[
            pltpu.VMEM((PB, col_count), jnp.bfloat16),
            pltpu.VMEM((PB, col_count), jnp.bfloat16),
            pltpu.VMEM((PB, target_width), jnp.float32),
            pltpu.VMEM((PB, target_width), jnp.bfloat16),
            pltpu.VMEM((PB, target_width), jnp.bfloat16),
        ],
        compiler_params=pltpu.CompilerParams(vmem_limit_bytes=40 * 1024 * 1024),
        name="update",
    )(
        covariance,
        row_raw,
        targets,
        noise_rows.reshape(row_count // ROWS, 1, ROWS),
        col_raw,
        head_raw,
        need_raw,
        factor,
        inverse,
        target_cov,
    )


def solution(mesh):
    placed = (P("row", "col"), P("row"), P(), P("row", "col"), P(), P(), P(), P())
    return jax.shard_map(
        functools.partial(local, mesh.shape["row"], mesh.shape["col"]),
        mesh=mesh,
        in_specs=placed,
        out_specs=(P("row", "col"), P("row", None), P("row", "col"), P("row", "col")),
        check_vma=False,
    )
```

```python
import functools

import jax
import jax.numpy as jnp
from jax import lax
from jax.experimental import pallas as pl
from jax.experimental.pallas import tpu as pltpu
from jax.sharding import PartitionSpec as P

PB = 256
TILE = 128
HALF = PB // 2
CHUNKS = 8
ROW_CHUNKS = 6
SEGMENT = 16

MESH = pl.DeviceIdType.MESH
precise = lax.Precision.HIGHEST


def dot(a, b, dims=((1,), (0,))):
    return lax.dot_general(
        a, b, (dims, ((), ())), precision=precise, preferred_element_type=jnp.float32
    )


def chunks_of(count):
    return max(n for n in range(1, CHUNKS + 1) if count // 128 % n == 0)


def split(x):
    high = x.astype(jnp.bfloat16)
    return high, (x - high.astype(jnp.float32)).astype(jnp.bfloat16)


def dot_split(a, b):
    total = jnp.dot(a[0], b[0], preferred_element_type=jnp.float32)
    total += jnp.dot(a[1], b[0], preferred_element_type=jnp.float32)
    return total + jnp.dot(a[0], b[1], preferred_element_type=jnp.float32)


def target_covariance(out, pos, strength, inverse_square, tile_layer, row_start, col_start):
    height, width = out.shape
    levels = strength.shape[0]

    def upright(axis):
        line = pos[pl.ds(axis, 1), pl.ds(row_start, height)]
        return jnp.broadcast_to(line, (TILE, height)).T

    rows = [upright(0), upright(1)]
    for i in range(height // TILE):
        for j in range(width // TILE):
            columns = pl.ds(pl.multiple_of(col_start + j * TILE, TILE), TILE)
            across = rows[0][i * TILE : (i + 1) * TILE] - pos[pl.ds(0, 1), columns]
            along = rows[1][i * TILE : (i + 1) * TILE] - pos[pl.ds(1, 1), columns]
            distance = across * across + along * along
            lowest = jnp.minimum(
                tile_layer[row_start // TILE + i], tile_layer[col_start // TILE + j]
            )

            def layer(l, total, distance=distance, lowest=lowest):
                weight = jnp.where(l <= lowest, strength[l], 0.0)
                return total + weight / (1.0 + distance * inverse_square[l])

            out[pl.ds(i * TILE, TILE), pl.ds(j * TILE, TILE)] = lax.fori_loop(
                0, levels, layer, jnp.zeros_like(distance)
            )


def gray_neighbours(c, n):
    position = c * 0
    after = c * 0
    before = c * 0
    ring = [i ^ (i >> 1) for i in range(n)]
    for i, node in enumerate(ring):
        position = jnp.where(c == node, i, position)
        after = jnp.where(c == node, ring[(i + 1) % n], after)
        before = jnp.where(c == node, ring[(i - 1) % n], before)
    return position, after, before


def pivots(t_ref, start, count):
    n = t_ref.shape[0]
    lanes = lax.broadcasted_iota(jnp.int32, (8, n), 1)
    wide = lax.broadcasted_iota(jnp.int32, (8, 2 * n), 1)
    down = lax.broadcasted_iota(jnp.int32, (8, 1), 0)

    def step(i, carry):
        k = pl.multiple_of(i * 8, 8)
        rows = t_ref[pl.ds(k, 8), :]
        left = rows[:, :n]
        columns = [
            jnp.sum(jnp.where(lanes == k + j, left, 0.0), axis=1, keepdims=True)
            for j in range(8)
        ]
        scale = jnp.ones((8, 1), jnp.float32)
        for j in range(8):
            pivot = columns[j][j : j + 1]
            scale = jnp.where(down == j, lax.rsqrt(pivot), scale)
            if j < 7:
                factor = jnp.where(down > j, columns[j] * (1.0 / pivot), 0.0)
                rows = rows - factor * rows[j : j + 1]
                for later in range(j + 1, 8):
                    columns[later] = columns[later] - factor * columns[later][j : j + 1]
        rows = rows * scale
        rows = jnp.where((wide >= n) | (wide >= k + down), rows, 0.0)
        below = jnp.where(lanes >= k + 8, rows[:, :n], 0.0)
        t_ref[...] = t_ref[...] - dot(below, rows, ((0,), (0,)))
        t_ref[pl.ds(k, 8), :] = rows
        return carry

    lax.fori_loop(start // 8, (start + count) // 8, step, 0)


def exchange_kernel(
    n_row,
    n_col,
    cov,
    targets,
    diag,
    pos,
    strength,
    inverse_square,
    tile_layer,
    row_raw,
    col_raw,
    head_raw,
    need_raw,
    factor_ref,
    inverse_ref,
    target_cov,
    blocks,
    t_ref,
    local_sem,
    diag_send,
    diag_recv,
    col_send,
    col_recv,
    row_send,
    row_recv,
    need_send,
    need_recv,
):
    r = lax.axis_index("row")
    c = lax.axis_index("col")
    row_count = row_raw.shape[0]
    col_count = col_raw.shape[1]
    width = head_raw.shape[1]
    need = need_raw.shape[1]
    col_chunks = chunks_of(col_count)
    even = lax.rem(r, 2) == 0
    place, after, before = gray_neighbours(c, n_col)
    far_row = jnp.minimum(r + 2, n_row - 1)
    near_row = jnp.where(even, r + 1, r - 1)

    head_copy = pltpu.make_async_copy(targets.at[pl.ds(0, PB), :], head_raw, local_sem.at[0])
    col_copy = pltpu.make_async_copy(cov.at[pl.ds(0, PB), :], col_raw, local_sem.at[1])
    row_copy = pltpu.make_async_copy(cov.at[:, pl.ds(0, PB)], row_raw, local_sem.at[2])
    pl.when(r == 0)(lambda: (head_copy.start(), col_copy.start(), None)[-1])
    pl.when(c == 0)(lambda: (row_copy.start(), None)[-1])

    barrier = pltpu.get_barrier_semaphore()
    for k in range(1, n_row):
        pl.semaphore_signal(
            barrier, inc=1, device_id=(c, lax.rem(r + k, n_row)), device_id_type=MESH
        )
    for k in range(1, n_col):
        pl.semaphore_signal(
            barrier, inc=1, device_id=(lax.rem(c + k, n_col), r), device_id_type=MESH
        )
    pl.semaphore_wait(barrier, n_row + n_col - 2)

    def remote(src, dst, send, recv, col, row):
        return pltpu.make_async_remote_copy(
            src_ref=src,
            dst_ref=dst,
            send_sem=send,
            recv_sem=recv,
            device_id=(col, row),
            device_id_type=MESH,
        )

    def chain(src, dst, send, recv):
        return (
            remote(src, dst, send.at[0], recv, c, far_row),
            remote(src, dst, send.at[1], recv, c, near_row),
        )

    def chain_start(copies, allowed):
        pl.when(allowed & even & (r + 2 < n_row))(lambda: (copies[0].start(), None)[-1])
        pl.when(allowed & even & (r + 1 < n_row))(lambda: (copies[1].start(), None)[-1])

    def chain_end(copies, allowed):
        pl.when(allowed & even & (r + 2 < n_row))(lambda: (copies[0].wait_send(), None)[-1])
        pl.when(allowed & even & (r + 1 < n_row))(lambda: (copies[1].wait_send(), None)[-1])

    quarters = [(0, 0), (HALF, 0), (HALF, HALF)]

    def diag_chain(i, source):
        dst = blocks.at[i]
        src = dst
        if source:
            src = diag.at[pl.ds(quarters[i][0], HALF), pl.ds(quarters[i][1], HALF)]
        return src, dst

    def diag_copies(i, source):
        src, dst = diag_chain(i, source)
        down = chain(src, dst, diag_send.at[i], diag_recv.at[i])
        across = [
            remote(src, dst, diag_send.at[i, 1 + k], diag_recv.at[i], k, r)
            for k in range(1, n_col)
        ]
        return down, across

    def diag_start(i, source, allowed):
        down, across = diag_copies(i, source)
        chain_start(down, allowed)
        for copy in across:
            pl.when(allowed)(lambda copy=copy: (copy.start(), None)[-1])

    def diag_wait(i):
        @pl.when((r > 0) | (c > 0))
        def _():
            diag_copies(i, False)[0][0].wait_recv()

    first = (r == 0) & (c == 0)
    for i in range(3):
        diag_start(i, True, first)

    chunk = col_count // col_chunks

    def col_copies(j, source):
        if j == 0:
            src = targets.at[pl.ds(0, PB), :] if source else head_raw
            return chain(src, head_raw, col_send.at[j], col_recv.at[j])
        columns = pl.ds((j - 1) * chunk, chunk)
        dst = col_raw.at[:, columns]
        src = cov.at[pl.ds(0, PB), columns] if source else dst
        return chain(src, dst, col_send.at[j], col_recv.at[j])

    def col_forward(j):
        @pl.when((r > 0) & even)
        def _():
            col_copies(j, False)[0].wait_recv()

        chain_start(col_copies(j, False), r > 0)

    target_covariance(
        target_cov,
        pos,
        strength,
        inverse_square,
        tile_layer,
        pl.multiple_of(r * need, 128),
        pl.multiple_of(c * width, 128),
    )

    for i in range(3):
        diag_wait(i)
        diag_start(i, False, (r > 0) & (c == 0))

    for j in range(col_chunks + 1):
        chain_start(col_copies(j, True), r == 0)

    step_rows = row_count // (2 * ROW_CHUNKS)

    def row_copies(j, way, source):
        rows = pl.ds((2 * j + way) * step_rows, step_rows)
        dst = row_raw.at[rows, :]
        src = cov.at[rows, pl.ds(0, PB)] if source else dst
        to = after if way == 0 else before
        return remote(src, dst, row_send.at[j, way], row_recv.at[j, way], to, r)

    def forwards(way):
        return (place > 0) & ((place < n_col - 1) if way == 0 else (place > 1))

    def row_forward(j):
        for way in range(2):
            copy = row_copies(j, way, False)
            pl.when(forwards(way))(lambda copy=copy: (copy.wait_recv(), copy.start(), None)[-1])

    for j in range(ROW_CHUNKS):
        for way in range(2):
            copy = row_copies(j, way, True)
            pl.when(place == 0)(lambda copy=copy: (copy.start(), None)[-1])

    owner = lax.div(r * need, width)
    offset = pl.multiple_of(lax.rem(r * need, width), 128)
    need_copies = [
        remote(
            head_raw.at[:, pl.ds(offset, need)], need_raw, need_send.at[k], need_recv, k, r
        )
        for k in range(n_col)
    ]
    own_need = pltpu.make_async_copy(
        head_raw.at[:, pl.ds(offset, need)], need_raw, local_sem.at[3]
    )

    def need_start():
        pl.when(r == 0)(lambda: (head_copy.wait(), None)[-1])
        pl.when((r > 0) & ~even & (c == owner))(
            lambda: (col_copies(0, False)[0].wait_recv(), None)[-1]
        )
        for k in range(n_col):
            pl.when((c == owner) & (c != k))(lambda k=k: (need_copies[k].start(), None)[-1])
        pl.when(c == owner)(lambda: (own_need.start(), None)[-1])

    @pl.when(first)
    def _():
        for i in range(3):
            blocks[i] = diag[pl.ds(quarters[i][0], HALF), pl.ds(quarters[i][1], HALF)]

    unit = (
        lax.broadcasted_iota(jnp.int32, (HALF, HALF), 0)
        == lax.broadcasted_iota(jnp.int32, (HALF, HALF), 1)
    ).astype(jnp.float32)
    events = [lambda: row_forward(0), lambda: (col_forward(0), need_start(), row_forward(1))]
    for j in range(max(col_chunks, ROW_CHUNKS)):
        if j + 2 < ROW_CHUNKS:
            events.append(lambda j=j: row_forward(j + 2))
        if j < col_chunks:
            events.append(lambda j=j: col_forward(j + 1))

    def half(block, where):
        t_ref[:, pl.ds(0, HALF)] = block
        t_ref[:, pl.ds(HALF, HALF)] = unit
        for start in range(0, HALF, SEGMENT):
            pivots(t_ref, start, SEGMENT)
            if events:
                events.pop(0)()

    half(blocks[0], 0)
    inverse_11 = t_ref[:, pl.ds(HALF, HALF)]
    inverse_ref[pl.ds(0, HALF), pl.ds(0, HALF)] = inverse_11
    inverse_ref[pl.ds(0, HALF), pl.ds(HALF, HALF)] = jnp.zeros((HALF, HALF), jnp.float32)
    factor_ref[pl.ds(0, HALF), pl.ds(0, HALF)] = t_ref[:, pl.ds(0, HALF)].T
    factor_ref[pl.ds(0, HALF), pl.ds(HALF, HALF)] = jnp.zeros((HALF, HALF), jnp.float32)
    lower = dot(blocks[1], inverse_11, ((1,), (1,)))
    factor_ref[pl.ds(HALF, HALF), pl.ds(0, HALF)] = lower
    half(blocks[2] - dot(lower, lower, ((1,), (1,))), 1)
    inverse_22 = t_ref[:, pl.ds(HALF, HALF)]
    inverse_ref[pl.ds(HALF, HALF), pl.ds(HALF, HALF)] = inverse_22
    factor_ref[pl.ds(HALF, HALF), pl.ds(HALF, HALF)] = t_ref[:, pl.ds(0, HALF)].T
    lower = factor_ref[pl.ds(HALF, HALF), pl.ds(0, HALF)]
    inverse_ref[pl.ds(HALF, HALF), pl.ds(0, HALF)] = -dot(
        inverse_22, dot(lower, inverse_ref[pl.ds(0, HALF), pl.ds(0, HALF)])
    )
    while events:
        events.pop(0)()

    for j in range(col_chunks + 1):
        late = ~even & (c != owner) if j == 0 else ~even
        pl.when(late)(lambda j=j: (col_copies(j, False)[0].wait_recv(), None)[-1])
    for j in range(ROW_CHUNKS):
        for way in range(2):
            copy = row_copies(j, way, False)
            pl.when((place > 0) & ~forwards(way))(lambda copy=copy: (copy.wait_recv(), None)[-1])
    pl.when(c == owner)(lambda: (own_need.wait(), None)[-1])
    pl.when(c != owner)(lambda: (need_copies[0].wait_recv(), None)[-1])
    for k in range(n_col):
        pl.when((c == owner) & (c != k))(lambda k=k: (need_copies[k].wait_send(), None)[-1])
    for i in range(3):
        down, across = diag_copies(i, True)
        chain_end(down, c == 0)
        for copy in across:
            pl.when(c == 0)(lambda copy=copy: (copy.wait_send(), None)[-1])
    for j in range(col_chunks + 1):
        chain_end(col_copies(j, False), r >= 0)
    for j in range(ROW_CHUNKS):
        for way in range(2):
            copy = row_copies(j, way, False)
            pl.when((place == 0) | forwards(way))(lambda copy=copy: (copy.wait_send(), None)[-1])
    pl.when(r == 0)(lambda: (col_copy.wait(), None)[-1])
    pl.when(c == 0)(lambda: (row_copy.wait(), None)[-1])


def update_kernel(
    cov,
    row_raw,
    targets,
    noise,
    col_raw,
    head_raw,
    need_raw,
    factor,
    inverse,
    target_cov,
    updated,
    panel,
    reconstructor,
    error_cov,
    left,
    left_high,
    left_low,
    head,
    head_high,
    head_low,
):
    t = pl.program_id(0)
    r = lax.axis_index("row")
    c = lax.axis_index("col")
    rows, cols = cov.shape
    part = panel.shape[0]

    @pl.when(t == 0)
    def _():
        whole = inverse[...]
        solved = dot(row_raw[...], whole, ((1,), (1,)))
        left[...] = solved
        left_high[...], left_low[...] = split(solved)

        @pl.when(r == 0)
        def _():
            left[pl.ds(0, PB), :] = factor[...]

        solved = dot(whole, head_raw[...])
        head[...] = solved
        head_high[...], head_low[...] = split(solved)
        other = dot(whole, need_raw[...])
        error_cov[...] = target_cov[...] - dot(other, solved, ((0,), (0,)))

    here = pl.ds(pl.multiple_of(t * part, part), part)
    panel[...] = left[here, :]
    reconstructor[...] = targets[...] - dot_split(
        (left_high[here, :], left_low[here, :]), (head_high[...], head_low[...])
    )

    @pl.when((r == 0) & (t < PB // part))
    def _():
        block = pl.ds(pl.multiple_of(jnp.minimum(t, PB // part - 1) * part, part), part)
        reconstructor[...] = head[block, :]

    right = split(dot(inverse[...], col_raw[...]))
    updated[...] = cov[...] - dot_split((left_high[...], left_low[...]), right)
    start = c * (cols * pl.num_programs(0)) + t * cols - r * rows

    @pl.when((start >= 0) & (start < rows))
    def _():
        block = pl.ds(pl.multiple_of(start, cols), cols)
        diagonal = lax.broadcasted_iota(jnp.int32, (cols, cols), 0) == (
            lax.broadcasted_iota(jnp.int32, (cols, cols), 1)
        )
        updated[block, :] = updated[block, :] + jnp.where(diagonal, noise[start // cols], 0.0)

    @pl.when(r == 0)
    def _():
        updated[pl.ds(0, PB), :] = jnp.zeros((PB, cols), jnp.float32)

    @pl.when((c == 0) & (t == 0))
    def _():
        updated[...] = left[...]


def local(
    n_row, n_col, covariance, wfs_map, noise_var, targets, target_pos, layer_strength,
    layer_scale, tile_layer
):
    row_count, col_count = covariance.shape
    target_width = targets.shape[1]
    kinds = jnp.arange(noise_var.shape[0], dtype=jnp.int32)
    noise_rows = jnp.sum(
        jnp.where(wfs_map[None, :] == kinds[:, None], noise_var[:, None], 0.0), axis=0
    )
    diag = covariance[:PB, :PB] + jnp.where(
        jnp.arange(PB)[:, None] == jnp.arange(PB)[None, :], noise_rows[None, :PB], 0.0
    )
    error_rows = target_width * n_col // n_row
    col_chunks = chunks_of(col_count)
    def f32(*shape):
        return jax.ShapeDtypeStruct(shape, jnp.float32)

    vmem = pl.BlockSpec(memory_space=pltpu.VMEM)
    anywhere = pl.BlockSpec(memory_space=pltpu.HBM)
    smem = pl.BlockSpec(memory_space=pltpu.SMEM)
    dma = pltpu.SemaphoreType.DMA
    row_raw, col_raw, head_raw, need_raw, factor, inverse, target_cov = pl.pallas_call(
        functools.partial(exchange_kernel, n_row, n_col),
        out_shape=(
            f32(row_count, PB),
            f32(PB, col_count),
            f32(PB, target_width),
            f32(PB, error_rows),
            f32(PB, PB),
            f32(PB, PB),
            f32(error_rows, target_width),
        ),
        in_specs=[anywhere, anywhere, vmem, vmem, smem, smem, smem],
        out_specs=[vmem] * 7,
        scratch_shapes=[
            pltpu.VMEM((3, HALF, HALF), jnp.float32),
            pltpu.VMEM((HALF, PB), jnp.float32),
            dma((4,)),
            dma((3, n_col + 1)),
            dma((3,)),
            dma((col_chunks + 1, 2)),
            dma((col_chunks + 1,)),
            dma((ROW_CHUNKS, 2)),
            dma((ROW_CHUNKS, 2)),
            dma((n_col,)),
            dma,
        ],
        compiler_params=pltpu.CompilerParams(
            collective_id=0, has_side_effects=True, vmem_limit_bytes=52 * 1024 * 1024
        ),
        name="exchange",
    )(
        covariance,
        targets,
        diag,
        target_pos,
        layer_strength,
        1.0 / (layer_scale * layer_scale),
        tile_layer,
    )

    steps = col_count // PB
    part = row_count // steps

    def tiled(width):
        return pl.BlockSpec((part, width), lambda t: (t, 0))

    def across(height):
        return pl.BlockSpec((height, PB), lambda t: (0, t))

    def held(height, width):
        return pl.BlockSpec((height, width), lambda t: (0, 0))

    return pl.pallas_call(
        update_kernel,
        grid=(steps,),
        out_shape=(
            f32(row_count, col_count),
            f32(row_count, PB),
            f32(row_count, target_width),
            f32(error_rows, target_width),
        ),
        in_specs=[
            across(row_count),
            held(row_count, PB),
            tiled(target_width),
            pl.BlockSpec((row_count // PB, 1, PB), lambda t: (0, 0, 0)),
            across(PB),
            held(PB, target_width),
            held(PB, error_rows),
            held(PB, PB),
            held(PB, PB),
            held(error_rows, target_width),
        ],
        out_specs=[
            across(row_count),
            tiled(PB),
            tiled(target_width),
            held(error_rows, target_width),
        ],
        scratch_shapes=[
            pltpu.VMEM((row_count, PB), jnp.float32),
            pltpu.VMEM((row_count, PB), jnp.bfloat16),
            pltpu.VMEM((row_count, PB), jnp.bfloat16),
            pltpu.VMEM((PB, target_width), jnp.float32),
            pltpu.VMEM((PB, target_width), jnp.bfloat16),
            pltpu.VMEM((PB, target_width), jnp.bfloat16),
        ],
        compiler_params=pltpu.CompilerParams(vmem_limit_bytes=40 * 1024 * 1024),
        name="update",
    )(
        covariance,
        row_raw,
        targets,
        noise_rows.reshape(row_count // PB, 1, PB),
        col_raw,
        head_raw,
        need_raw,
        factor,
        inverse,
        target_cov,
    )


def solution(mesh):
    placed = (P("row", "col"), P("row"), P(), P("row", "col"), P(), P(), P(), P())
    return jax.shard_map(
        functools.partial(local, mesh.shape["row"], mesh.shape["col"]),
        mesh=mesh,
        in_specs=placed,
        out_specs=(P("row", "col"), P("row", None), P("row", "col"), P("row", "col")),
        check_vma=False,
    )
```

```python
import functools

import jax
import jax.numpy as jnp
from jax import lax
from jax.experimental import pallas as pl
from jax.experimental.pallas import tpu as pltpu
from jax.sharding import PartitionSpec as P

PB = 256
TILE = 128
HALF = PB // 2
CHUNKS = 8
ROW_CHUNKS = 6
SEGMENT = 16

MESH = pl.DeviceIdType.MESH
precise = lax.Precision.HIGHEST


def dot(a, b, dims=((1,), (0,))):
    return lax.dot_general(
        a, b, (dims, ((), ())), precision=precise, preferred_element_type=jnp.float32
    )


def outer(a, b):
    def thirds(x):
        high = x.astype(jnp.bfloat16).astype(jnp.float32)
        middle = (x - high).astype(jnp.bfloat16).astype(jnp.float32)
        return high, middle, x - high - middle

    p, q = thirds(a), thirds(b)
    left = jnp.concatenate([p[0], p[0], p[1], p[0], p[2], p[1]], axis=0)
    right = jnp.concatenate([q[0], q[1], q[0], q[2], q[0], q[1]], axis=0)
    return lax.dot_general(
        left.astype(jnp.bfloat16),
        right.astype(jnp.bfloat16),
        (((0,), (0,)), ((), ())),
        preferred_element_type=jnp.float32,
    )


def chunks_of(count):
    return max(n for n in range(1, CHUNKS + 1) if count // 128 % n == 0)


def split(x):
    high = x.astype(jnp.bfloat16)
    return high, (x - high.astype(jnp.float32)).astype(jnp.bfloat16)


def target_covariance(out, pos, strength, inverse_square, tile_layer, row_start, col_start):
    height, width = out.shape
    levels = strength.shape[0]

    def upright(axis):
        line = pos[pl.ds(axis, 1), pl.ds(row_start, height)]
        return jnp.broadcast_to(line, (TILE, height)).T

    rows = [upright(0), upright(1)]
    for i in range(height // TILE):
        for j in range(width // TILE):
            columns = pl.ds(pl.multiple_of(col_start + j * TILE, TILE), TILE)
            across = rows[0][i * TILE : (i + 1) * TILE] - pos[pl.ds(0, 1), columns]
            along = rows[1][i * TILE : (i + 1) * TILE] - pos[pl.ds(1, 1), columns]
            distance = across * across + along * along
            lowest = jnp.minimum(
                tile_layer[row_start // TILE + i], tile_layer[col_start // TILE + j]
            )

            def layer(l, total, distance=distance, lowest=lowest):
                weight = jnp.where(l <= lowest, strength[l], 0.0)
                return total + weight / (1.0 + distance * inverse_square[l])

            out[pl.ds(i * TILE, TILE), pl.ds(j * TILE, TILE)] = lax.fori_loop(
                0, levels, layer, jnp.zeros_like(distance)
            )


def gray_neighbours(c, n):
    position = c * 0
    after = c * 0
    before = c * 0
    ring = [i ^ (i >> 1) for i in range(n)]
    for i, node in enumerate(ring):
        position = jnp.where(c == node, i, position)
        after = jnp.where(c == node, ring[(i + 1) % n], after)
        before = jnp.where(c == node, ring[(i - 1) % n], before)
    return position, after, before


def pivots(t_ref, start, count):
    n = t_ref.shape[0]
    lanes = lax.broadcasted_iota(jnp.int32, (8, n), 1)
    wide = lax.broadcasted_iota(jnp.int32, (8, 2 * n), 1)
    down = lax.broadcasted_iota(jnp.int32, (8, 1), 0)

    def step(i, carry):
        k = pl.multiple_of(i * 8, 8)
        rows = t_ref[pl.ds(k, 8), :]
        left = rows[:, :n]
        columns = [
            jnp.sum(jnp.where(lanes == k + j, left, 0.0), axis=1, keepdims=True)
            for j in range(8)
        ]
        scale = jnp.ones((8, 1), jnp.float32)
        for j in range(8):
            pivot = columns[j][j : j + 1]
            scale = jnp.where(down == j, lax.rsqrt(pivot), scale)
            if j < 7:
                factor = jnp.where(down > j, columns[j] * (1.0 / pivot), 0.0)
                rows = rows - factor * rows[j : j + 1]
                for later in range(j + 1, 8):
                    columns[later] = columns[later] - factor * columns[later][j : j + 1]
        rows = rows * scale
        rows = jnp.where((wide >= n) | (wide >= k + down), rows, 0.0)
        below = jnp.where(lanes >= k + 8, rows[:, :n], 0.0)
        t_ref[...] = t_ref[...] - outer(below, rows)
        t_ref[pl.ds(k, 8), :] = rows
        return carry

    lax.fori_loop(start // 8, (start + count) // 8, step, 0)


def exchange_kernel(
    n_row,
    n_col,
    cov,
    targets,
    diag,
    pos,
    strength,
    inverse_square,
    tile_layer,
    row_raw,
    col_raw,
    head_raw,
    need_raw,
    factor_ref,
    inverse_ref,
    target_cov,
    blocks,
    t_ref,
    local_sem,
    diag_send,
    diag_recv,
    col_send,
    col_recv,
    row_send,
    row_recv,
    need_send,
    need_recv,
):
    r = lax.axis_index("row")
    c = lax.axis_index("col")
    row_count = row_raw.shape[0]
    col_count = col_raw.shape[1]
    width = head_raw.shape[1]
    need = need_raw.shape[1]
    col_chunks = chunks_of(col_count)
    even = lax.rem(r, 2) == 0
    place, after, before = gray_neighbours(c, n_col)
    far_row = jnp.minimum(r + 2, n_row - 1)
    near_row = jnp.where(even, r + 1, r - 1)

    head_copy = pltpu.make_async_copy(targets.at[pl.ds(0, PB), :], head_raw, local_sem.at[0])
    col_copy = pltpu.make_async_copy(cov.at[pl.ds(0, PB), :], col_raw, local_sem.at[1])
    row_copy = pltpu.make_async_copy(cov.at[:, pl.ds(0, PB)], row_raw, local_sem.at[2])
    pl.when(r == 0)(lambda: (head_copy.start(), col_copy.start(), None)[-1])
    pl.when(c == 0)(lambda: (row_copy.start(), None)[-1])

    barrier = pltpu.get_barrier_semaphore()
    for k in range(1, n_row):
        pl.semaphore_signal(
            barrier, inc=1, device_id=(c, lax.rem(r + k, n_row)), device_id_type=MESH
        )
    for k in range(1, n_col):
        pl.semaphore_signal(
            barrier, inc=1, device_id=(lax.rem(c + k, n_col), r), device_id_type=MESH
        )
    pl.semaphore_wait(barrier, n_row + n_col - 2)

    def remote(src, dst, send, recv, col, row):
        return pltpu.make_async_remote_copy(
            src_ref=src,
            dst_ref=dst,
            send_sem=send,
            recv_sem=recv,
            device_id=(col, row),
            device_id_type=MESH,
        )

    def chain(src, dst, send, recv):
        return (
            remote(src, dst, send.at[0], recv, c, far_row),
            remote(src, dst, send.at[1], recv, c, near_row),
        )

    def chain_start(copies, allowed):
        pl.when(allowed & even & (r + 2 < n_row))(lambda: (copies[0].start(), None)[-1])
        pl.when(allowed & even & (r + 1 < n_row))(lambda: (copies[1].start(), None)[-1])

    def chain_end(copies, allowed):
        pl.when(allowed & even & (r + 2 < n_row))(lambda: (copies[0].wait_send(), None)[-1])
        pl.when(allowed & even & (r + 1 < n_row))(lambda: (copies[1].wait_send(), None)[-1])

    quarters = [(0, 0), (HALF, 0), (HALF, HALF)]

    def diag_chain(i, source):
        dst = blocks.at[i]
        src = dst
        if source:
            src = diag.at[pl.ds(quarters[i][0], HALF), pl.ds(quarters[i][1], HALF)]
        return src, dst

    def diag_copies(i, source):
        src, dst = diag_chain(i, source)
        down = chain(src, dst, diag_send.at[i], diag_recv.at[i])
        across = [
            remote(src, dst, diag_send.at[i, 1 + k], diag_recv.at[i], k, r)
            for k in range(1, n_col)
        ]
        return down, across

    def diag_start(i, source, allowed):
        down, across = diag_copies(i, source)
        chain_start(down, allowed)
        for copy in across:
            pl.when(allowed)(lambda copy=copy: (copy.start(), None)[-1])

    def diag_wait(i):
        @pl.when((r > 0) | (c > 0))
        def _():
            diag_copies(i, False)[0][0].wait_recv()

    first = (r == 0) & (c == 0)
    for i in range(3):
        diag_start(i, True, first)

    chunk = col_count // col_chunks

    def col_copies(j, source):
        if j == 0:
            src = targets.at[pl.ds(0, PB), :] if source else head_raw
            return chain(src, head_raw, col_send.at[j], col_recv.at[j])
        columns = pl.ds((j - 1) * chunk, chunk)
        dst = col_raw.at[:, columns]
        src = cov.at[pl.ds(0, PB), columns] if source else dst
        return chain(src, dst, col_send.at[j], col_recv.at[j])

    def col_forward(j):
        @pl.when((r > 0) & even)
        def _():
            col_copies(j, False)[0].wait_recv()

        chain_start(col_copies(j, False), r > 0)

    target_covariance(
        target_cov,
        pos,
        strength,
        inverse_square,
        tile_layer,
        pl.multiple_of(r * need, 128),
        pl.multiple_of(c * width, 128),
    )

    for i in range(3):
        diag_wait(i)
        diag_start(i, False, (r > 0) & (c == 0))

    for j in range(col_chunks + 1):
        chain_start(col_copies(j, True), r == 0)

    step_rows = row_count // (2 * ROW_CHUNKS)

    def row_copies(j, way, source):
        rows = pl.ds((2 * j + way) * step_rows, step_rows)
        dst = row_raw.at[rows, :]
        src = cov.at[rows, pl.ds(0, PB)] if source else dst
        to = after if way == 0 else before
        return remote(src, dst, row_send.at[j, way], row_recv.at[j, way], to, r)

    def forwards(way):
        return (place > 0) & ((place < n_col - 1) if way == 0 else (place > 1))

    def row_forward(j):
        for way in range(2):
            copy = row_copies(j, way, False)
            pl.when(forwards(way))(lambda copy=copy: (copy.wait_recv(), copy.start(), None)[-1])

    for j in range(ROW_CHUNKS):
        for way in range(2):
            copy = row_copies(j, way, True)
            pl.when(place == 0)(lambda copy=copy: (copy.start(), None)[-1])

    owner = lax.div(r * need, width)
    offset = pl.multiple_of(lax.rem(r * need, width), 128)
    need_copies = [
        remote(
            head_raw.at[:, pl.ds(offset, need)], need_raw, need_send.at[k], need_recv, k, r
        )
        for k in range(n_col)
    ]
    own_need = pltpu.make_async_copy(
        head_raw.at[:, pl.ds(offset, need)], need_raw, local_sem.at[3]
    )

    def need_start():
        pl.when(r == 0)(lambda: (head_copy.wait(), None)[-1])
        pl.when((r > 0) & ~even & (c == owner))(
            lambda: (col_copies(0, False)[0].wait_recv(), None)[-1]
        )
        for k in range(n_col):
            pl.when((c == owner) & (c != k))(lambda k=k: (need_copies[k].start(), None)[-1])
        pl.when(c == owner)(lambda: (own_need.start(), None)[-1])

    @pl.when(first)
    def _():
        for i in range(3):
            blocks[i] = diag[pl.ds(quarters[i][0], HALF), pl.ds(quarters[i][1], HALF)]

    unit = (
        lax.broadcasted_iota(jnp.int32, (HALF, HALF), 0)
        == lax.broadcasted_iota(jnp.int32, (HALF, HALF), 1)
    ).astype(jnp.float32)
    events = [lambda: row_forward(0), lambda: (col_forward(0), need_start(), row_forward(1))]
    for j in range(max(col_chunks, ROW_CHUNKS)):
        if j + 2 < ROW_CHUNKS:
            events.append(lambda j=j: row_forward(j + 2))
        if j < col_chunks:
            events.append(lambda j=j: col_forward(j + 1))

    def half(block, where):
        t_ref[:, pl.ds(0, HALF)] = block
        t_ref[:, pl.ds(HALF, HALF)] = unit
        for start in range(0, HALF, SEGMENT):
            pivots(t_ref, start, SEGMENT)
            if events:
                events.pop(0)()

    half(blocks[0], 0)
    inverse_11 = t_ref[:, pl.ds(HALF, HALF)]
    inverse_ref[pl.ds(0, HALF), pl.ds(0, HALF)] = inverse_11
    inverse_ref[pl.ds(0, HALF), pl.ds(HALF, HALF)] = jnp.zeros((HALF, HALF), jnp.float32)
    factor_ref[pl.ds(0, HALF), pl.ds(0, HALF)] = t_ref[:, pl.ds(0, HALF)].T
    factor_ref[pl.ds(0, HALF), pl.ds(HALF, HALF)] = jnp.zeros((HALF, HALF), jnp.float32)
    lower = dot(blocks[1], inverse_11, ((1,), (1,)))
    factor_ref[pl.ds(HALF, HALF), pl.ds(0, HALF)] = lower
    half(blocks[2] - dot(lower, lower, ((1,), (1,))), 1)
    inverse_22 = t_ref[:, pl.ds(HALF, HALF)]
    inverse_ref[pl.ds(HALF, HALF), pl.ds(HALF, HALF)] = inverse_22
    factor_ref[pl.ds(HALF, HALF), pl.ds(HALF, HALF)] = t_ref[:, pl.ds(0, HALF)].T
    lower = factor_ref[pl.ds(HALF, HALF), pl.ds(0, HALF)]
    inverse_ref[pl.ds(HALF, HALF), pl.ds(0, HALF)] = -dot(
        inverse_22, dot(lower, inverse_ref[pl.ds(0, HALF), pl.ds(0, HALF)])
    )
    while events:
        events.pop(0)()

    for j in range(col_chunks + 1):
        late = ~even & (c != owner) if j == 0 else ~even
        pl.when(late)(lambda j=j: (col_copies(j, False)[0].wait_recv(), None)[-1])
    for j in range(ROW_CHUNKS):
        for way in range(2):
            copy = row_copies(j, way, False)
            pl.when((place > 0) & ~forwards(way))(lambda copy=copy: (copy.wait_recv(), None)[-1])
    pl.when(c == owner)(lambda: (own_need.wait(), None)[-1])
    pl.when(c != owner)(lambda: (need_copies[0].wait_recv(), None)[-1])
    for k in range(n_col):
        pl.when((c == owner) & (c != k))(lambda k=k: (need_copies[k].wait_send(), None)[-1])
    for i in range(3):
        down, across = diag_copies(i, True)
        chain_end(down, c == 0)
        for copy in across:
            pl.when(c == 0)(lambda copy=copy: (copy.wait_send(), None)[-1])
    for j in range(col_chunks + 1):
        chain_end(col_copies(j, False), r >= 0)
    for j in range(ROW_CHUNKS):
        for way in range(2):
            copy = row_copies(j, way, False)
            pl.when((place == 0) | forwards(way))(lambda copy=copy: (copy.wait_send(), None)[-1])
    pl.when(r == 0)(lambda: (col_copy.wait(), None)[-1])
    pl.when(c == 0)(lambda: (row_copy.wait(), None)[-1])


def update_kernel(
    cov,
    row_raw,
    targets,
    noise,
    col_raw,
    head_raw,
    need_raw,
    factor,
    inverse,
    target_cov,
    updated,
    panel,
    reconstructor,
    error_cov,
    left,
    left_parts,
    head,
    head_parts,
):
    t = pl.program_id(0)
    r = lax.axis_index("row")
    c = lax.axis_index("col")
    rows, cols = cov.shape
    part = panel.shape[0]

    @pl.when(t == 0)
    def _():
        whole = inverse[...]
        solved = dot(row_raw[...], whole, ((1,), (1,)))
        left[...] = solved
        high, low = split(solved)
        left_parts[:, pl.ds(0, PB)] = high
        left_parts[:, pl.ds(PB, PB)] = low
        left_parts[:, pl.ds(2 * PB, PB)] = high

        @pl.when(r == 0)
        def _():
            left[pl.ds(0, PB), :] = factor[...]

        solved = dot(whole, head_raw[...])
        head[...] = solved
        high, low = split(solved)
        head_parts[...] = jnp.concatenate([high, high, low], axis=0)
        other = dot(whole, need_raw[...])
        error_cov[...] = target_cov[...] - dot(other, solved, ((0,), (0,)))

    here = pl.ds(pl.multiple_of(t * part, part), part)
    panel[...] = left[here, :]
    reconstructor[...] = targets[...] - jnp.dot(
        left_parts[here, :], head_parts[...], preferred_element_type=jnp.float32
    )

    @pl.when((r == 0) & (t < PB // part))
    def _():
        block = pl.ds(pl.multiple_of(jnp.minimum(t, PB // part - 1) * part, part), part)
        reconstructor[...] = head[block, :]

    high, low = split(dot(inverse[...], col_raw[...]))
    updated[...] = cov[...] - jnp.dot(
        left_parts[...],
        jnp.concatenate([high, high, low], axis=0),
        preferred_element_type=jnp.float32,
    )
    start = c * (cols * pl.num_programs(0)) + t * cols - r * rows

    @pl.when((start >= 0) & (start < rows))
    def _():
        block = pl.ds(pl.multiple_of(start, cols), cols)
        diagonal = lax.broadcasted_iota(jnp.int32, (cols, cols), 0) == (
            lax.broadcasted_iota(jnp.int32, (cols, cols), 1)
        )
        updated[block, :] = updated[block, :] + jnp.where(diagonal, noise[start // cols], 0.0)

    @pl.when(r == 0)
    def _():
        updated[pl.ds(0, PB), :] = jnp.zeros((PB, cols), jnp.float32)

    @pl.when((c == 0) & (t == 0))
    def _():
        updated[...] = left[...]


def local(
    n_row, n_col, covariance, wfs_map, noise_var, targets, target_pos, layer_strength,
    layer_scale, tile_layer
):
    row_count, col_count = covariance.shape
    target_width = targets.shape[1]
    kinds = jnp.arange(noise_var.shape[0], dtype=jnp.int32)
    noise_rows = jnp.sum(
        jnp.where(wfs_map[None, :] == kinds[:, None], noise_var[:, None], 0.0), axis=0
    )
    diag = covariance[:PB, :PB] + jnp.where(
        jnp.arange(PB)[:, None] == jnp.arange(PB)[None, :], noise_rows[None, :PB], 0.0
    )
    error_rows = target_width * n_col // n_row
    col_chunks = chunks_of(col_count)
    def f32(*shape):
        return jax.ShapeDtypeStruct(shape, jnp.float32)

    vmem = pl.BlockSpec(memory_space=pltpu.VMEM)
    anywhere = pl.BlockSpec(memory_space=pltpu.HBM)
    smem = pl.BlockSpec(memory_space=pltpu.SMEM)
    dma = pltpu.SemaphoreType.DMA
    row_raw, col_raw, head_raw, need_raw, factor, inverse, target_cov = pl.pallas_call(
        functools.partial(exchange_kernel, n_row, n_col),
        out_shape=(
            f32(row_count, PB),
            f32(PB, col_count),
            f32(PB, target_width),
            f32(PB, error_rows),
            f32(PB, PB),
            f32(PB, PB),
            f32(error_rows, target_width),
        ),
        in_specs=[anywhere, anywhere, vmem, vmem, smem, smem, smem],
        out_specs=[vmem] * 7,
        scratch_shapes=[
            pltpu.VMEM((3, HALF, HALF), jnp.float32),
            pltpu.VMEM((HALF, PB), jnp.float32),
            dma((4,)),
            dma((3, n_col + 1)),
            dma((3,)),
            dma((col_chunks + 1, 2)),
            dma((col_chunks + 1,)),
            dma((ROW_CHUNKS, 2)),
            dma((ROW_CHUNKS, 2)),
            dma((n_col,)),
            dma,
        ],
        compiler_params=pltpu.CompilerParams(
            collective_id=0, has_side_effects=True, vmem_limit_bytes=46 * 1024 * 1024
        ),
        name="exchange",
    )(
        covariance,
        targets,
        diag,
        target_pos,
        layer_strength,
        1.0 / (layer_scale * layer_scale),
        tile_layer,
    )

    steps = col_count // PB
    part = row_count // steps

    def tiled(width):
        return pl.BlockSpec((part, width), lambda t: (t, 0))

    def across(height):
        return pl.BlockSpec((height, PB), lambda t: (0, t))

    def held(height, width):
        return pl.BlockSpec((height, width), lambda t: (0, 0))

    return pl.pallas_call(
        update_kernel,
        grid=(steps,),
        out_shape=(
            f32(row_count, col_count),
            f32(row_count, PB),
            f32(row_count, target_width),
            f32(error_rows, target_width),
        ),
        in_specs=[
            across(row_count),
            held(row_count, PB),
            tiled(target_width),
            pl.BlockSpec((row_count // PB, 1, PB), lambda t: (0, 0, 0)),
            across(PB),
            held(PB, target_width),
            held(PB, error_rows),
            held(PB, PB),
            held(PB, PB),
            held(error_rows, target_width),
        ],
        out_specs=[
            across(row_count),
            tiled(PB),
            tiled(target_width),
            held(error_rows, target_width),
        ],
        scratch_shapes=[
            pltpu.VMEM((row_count, PB), jnp.float32),
            pltpu.VMEM((row_count, 3 * PB), jnp.bfloat16),
            pltpu.VMEM((PB, target_width), jnp.float32),
            pltpu.VMEM((3 * PB, target_width), jnp.bfloat16),
        ],
        compiler_params=pltpu.CompilerParams(vmem_limit_bytes=40 * 1024 * 1024),
        name="update",
    )(
        covariance,
        row_raw,
        targets,
        noise_rows.reshape(row_count // PB, 1, PB),
        col_raw,
        head_raw,
        need_raw,
        factor,
        inverse,
        target_cov,
    )


def solution(mesh):
    placed = (P("row", "col"), P("row"), P(), P("row", "col"), P(), P(), P(), P())
    return jax.shard_map(
        functools.partial(local, mesh.shape["row"], mesh.shape["col"]),
        mesh=mesh,
        in_specs=placed,
        out_specs=(P("row", "col"), P("row", None), P("row", "col"), P("row", "col")),
        check_vma=False,
    )
```
